32 devices in a mesh: pb: 2 (over x), ka: 16 (over z, y, core).
Axes of the slice: x: 2, y: 2, z: 4, core: 2. Of those that a mesh axis runs over, the one named last changes fastest.
Arguments:
- coupling: bfloat16 [5120, 2, 2048], P('ka', 'pb'), may hold values from -0.009765625 to 0.009765625
- eigvec: float32 [16, 2048], P('ka'), may hold values from -0.75 to 0.75
- energies: float32 [16, 32], P('ka'), may hold values from -1 to 1
- k_coords: int32 [3, 16], replicated, may hold values from 0 to 63
- r_coords: int32 [3, 5120], P(None, 'ka'), may hold values from -12 to 12
- degeneracy: int32 [5120], P('ka'), may hold values from 1 to 8
- kq_index: int32 [16, 24], P('ka', 'pb'), may hold values from 0 to 15
- omega: float32 [24, 2], P('pb'), may hold values from 0.05 to 0.5
- phonon_modes: float32 [24, 2, 2], P('pb'), may hold values from -4 to 4
Outputs:
- sigma: float32 [16, 32], P('ka', 'pb')
The draws below stay inside these ranges and needn't reach their ends.
All inputs are finite; a program needn't handle non-finite values.
Results may differ from the reference program's by a relative error of at most 0.0013.
Values may be sent and summed in bfloat16 or wider, within the bound.
No kernel may reach another device: no remote copies, remote signals or barrier semaphores. Data moves between devices by JAX's collectives and lax.ppermute only.
A program may use at most 64 MiB of HBM per device.

```python
import math
import jax
import jax.numpy as jnp
from jax import lax

NB = 32
KGRID = 64
RMAX = 12
NR = 5120
MODES = 2
KTOT = 16
QTOT = 24


def place_ends(entries, stream_key, smallest, high):
    extent = entries.shape
    spot = [jax.random.randint(jax.random.fold_in(stream_key, axis), (), 0, extent[axis]) for axis in range(len(extent))]
    entries = entries.at[tuple(spot)].set(smallest)
    longest = extent.index(max(extent))
    spot[longest] = (spot[longest] + 1) % extent[longest]
    return entries.at[tuple(spot)].set(high)


def block_levels(key, shape, split, low, largest):
    factor_of, own = 1.0, jax.random.fold_in(key, 6)
    for position, parts in split:
        steps = jnp.exp(jax.random.uniform(jax.random.fold_in(own, position), (parts,), jnp.float32, low / len(split), largest / len(split)))
        factor_of = factor_of * jnp.repeat(steps, shape[position] // parts).reshape([-1 if axis == position else 1 for axis in range(len(shape))])
    return factor_of


def normal_values(rng, extent, spread, reach, shards=(), kind=jnp.bfloat16):
    result = jax.random.normal(rng, extent, jnp.float32) * spread
    if len(shards) > 0:
        result = block_levels(rng, extent, shards, -0.22, 0.18) * result
    return jnp.clip(result, min=-reach, max=reach).astype(kind)


def setup_inputs(seed: int = 0) -> dict:
    seeds = jax.random.split(jax.random.key(seed), 10)
    coupling = normal_values(seeds[0], (NR, MODES, 2 * NB * NB), (NR * 64) ** -0.5, 0.009765625, ((0, 16), (1, 2)))
    eigvec = normal_values(seeds[1], (KTOT, 2 * NB * NB), (2 * NB) ** -0.5, 0.75, ((0, 16),), jnp.float32)
    energies = jnp.clip(jax.random.uniform(seeds[2], (KTOT, NB), jnp.float32, -1.0, 1.0) * block_levels(seeds[2], (KTOT, NB), ((0, 16),), -0.4, 0.0), -1.0, 1.0)
    k_coords = place_ends(jax.random.randint(seeds[3], (3, KTOT), 0, KGRID), jax.random.fold_in(seeds[3], 1), 0, KGRID - 1).astype(jnp.int32)
    r_coords = place_ends(jax.random.randint(seeds[4], (3, NR), 0 - RMAX, RMAX + 1), jax.random.fold_in(seeds[4], 1), 0 - RMAX, RMAX).astype(jnp.int32)
    degeneracy = place_ends(jax.random.randint(seeds[5], (NR,), 1, 9), jax.random.fold_in(seeds[5], 1), 1, 8).astype(jnp.int32)
    kq_index = place_ends(jax.random.randint(seeds[6], (KTOT, QTOT), 0, KTOT), jax.random.fold_in(seeds[6], 1), 0, KTOT - 1).astype(jnp.int32)
    omega = jnp.clip(jnp.exp(math.log(0.5) - 2.3025851 * jax.random.uniform(seeds[7], (QTOT, MODES), jnp.float32) ** block_levels(seeds[7], (QTOT, MODES), ((0, 2),), -0.2, 0.2)), 0.05, 0.5)
    phonon_modes = normal_values(seeds[8], (QTOT, MODES, MODES), MODES ** -0.5, 4.0, ((0, 2),), jnp.float32)
    return {"coupling": coupling, "eigvec": eigvec, "energies": energies, "k_coords": k_coords, "r_coords": r_coords, "degeneracy": degeneracy, "kq_index": kq_index, "omega": omega, "phonon_modes": phonon_modes}


THERMAL = 0.1
SMEARING = 0.05
HIGHEST = lax.Precision.HIGHEST


def phases(k_coords, r_coords, degeneracy):
    turns = (k_coords[0][:, None] * r_coords[0][None, :] + k_coords[1][:, None] * r_coords[1][None, :] + k_coords[2][:, None] * r_coords[2][None, :]) % KGRID
    angle = turns.astype(jnp.float32) * (2.0 * math.pi / KGRID)
    inverse = 1.0 / degeneracy.astype(jnp.float32)
    cosine = (jnp.cos(angle) * inverse[None, :]).astype(jnp.bfloat16)
    sine = (jnp.sin(angle) * inverse[None, :]).astype(jnp.bfloat16)
    return cosine, sine


def combine_parts(cosine_sum, sine_sum, modes, square):
    cosine_rows = cosine_sum.reshape(cosine_sum.shape[0], modes, 2, square)
    sine_rows = sine_sum.reshape(sine_sum.shape[0], modes, 2, square)
    real_part = cosine_rows[:, :, 0] - sine_rows[:, :, 1]
    imag_part = cosine_rows[:, :, 1] + sine_rows[:, :, 0]
    return jnp.stack([real_part, imag_part], axis=2).reshape(cosine_sum.shape[0], modes * 2 * square)


def lorentz(spacing):
    return SMEARING / (math.pi * (spacing * spacing + SMEARING * SMEARING))


def self_energy(wannier, vector, energy, kq_vectors, kq_energies, omega, phonon):
    bands = energy.shape[0]
    modes = wannier.shape[0]
    matrix = wannier.astype(jnp.float32).reshape(modes, 2, bands, bands)
    rotate = vector.reshape(2, bands, bands)
    fold_real = jnp.einsum("vac,cn->van", matrix[:, 0], rotate[0], precision=HIGHEST) - jnp.einsum("vac,cn->van", matrix[:, 1], rotate[1], precision=HIGHEST)
    fold_imag = jnp.einsum("vac,cn->van", matrix[:, 0], rotate[1], precision=HIGHEST) + jnp.einsum("vac,cn->van", matrix[:, 1], rotate[0], precision=HIGHEST)
    mixed_real = jnp.einsum("qwv,wan->qvan", phonon, fold_real, precision=HIGHEST)
    mixed_imag = jnp.einsum("qwv,wan->qvan", phonon, fold_imag, precision=HIGHEST)
    target = kq_vectors.reshape(-1, 2, bands, bands)
    final_real = jnp.einsum("qam,qvan->qmvn", target[:, 0], mixed_real, precision=HIGHEST) + jnp.einsum("qam,qvan->qmvn", target[:, 1], mixed_imag, precision=HIGHEST)
    final_imag = jnp.einsum("qam,qvan->qmvn", target[:, 0], mixed_imag, precision=HIGHEST) - jnp.einsum("qam,qvan->qmvn", target[:, 1], mixed_real, precision=HIGHEST)
    strength = final_real * final_real + final_imag * final_imag
    fermi = 1.0 / (1.0 + jnp.exp(kq_energies / THERMAL))
    bose = 1.0 / jnp.expm1(omega / THERMAL)
    spacing = energy[None, None, None, :] - kq_energies[:, :, None, None]
    absorb = lorentz(spacing + omega[:, None, :, None])
    emit = lorentz(spacing - omega[:, None, :, None])
    bose_wide = bose[:, None, :, None]
    fermi_wide = fermi[:, :, None, None]
    occupy = (bose_wide + fermi_wide) * absorb + (bose_wide + 1.0 - fermi_wide) * emit
    return jnp.sum(strength * occupy, axis=(0, 1, 2))


def reference(coupling, eigvec, energies, k_coords, r_coords, degeneracy, kq_index, omega, phonon_modes):
    cosine, sine = phases(k_coords, r_coords, degeneracy)
    flat = coupling.reshape(coupling.shape[0], -1)
    cosine_sum = jnp.dot(cosine, flat, preferred_element_type=jnp.float32)
    sine_sum = jnp.dot(sine, flat, preferred_element_type=jnp.float32)
    wannier = combine_parts(cosine_sum, sine_sum, MODES, NB * NB).astype(jnp.bfloat16)
    wannier = wannier.reshape(KTOT, MODES, 2 * NB * NB)

    def per_point(items):
        wannier_row, vector, energy, kq_row = items
        kq_vectors = eigvec[kq_row]
        kq_energies = energies[kq_row]
        return self_energy(wannier_row, vector, energy, kq_vectors, kq_energies, omega, phonon_modes)

    sigma = lax.map(per_point, (wannier, eigvec, energies, kq_index))
    return sigma / QTOT
```

```python
import math

import jax
import jax.numpy as jnp
from jax import lax
from jax.sharding import PartitionSpec as P

KGRID = 64


THERMAL = 0.1
SMEARING = 0.05
HIGHEST = lax.Precision.HIGHEST


def phases(k_coords, r_coords, degeneracy):
    turns = (
        k_coords[0][:, None] * r_coords[0][None, :]
        + k_coords[1][:, None] * r_coords[1][None, :]
        + k_coords[2][:, None] * r_coords[2][None, :]
    ) % KGRID
    angle = turns.astype(jnp.float32) * (2.0 * math.pi / KGRID)
    inverse = 1.0 / degeneracy.astype(jnp.float32)
    cosine = (jnp.cos(angle) * inverse[None, :]).astype(jnp.bfloat16)
    sine = (jnp.sin(angle) * inverse[None, :]).astype(jnp.bfloat16)
    return (cosine, sine)


def lorentz(spacing):
    return SMEARING / (math.pi * (spacing * spacing + SMEARING * SMEARING))


def fourier_terms(k_coords, r_coords, degeneracy, slab, modes, square):
    cosine, sine = phases(k_coords, r_coords, degeneracy)
    count = cosine.shape[0]
    stacked = jnp.dot(
        jnp.concatenate([cosine, sine], axis=0), slab, preferred_element_type=jnp.float32
    ).reshape(2, count, modes, 2, square)
    real_part = stacked[0, :, :, 0] - stacked[1, :, :, 1]
    imag_part = stacked[0, :, :, 1] + stacked[1, :, :, 0]
    return jnp.stack([real_part, imag_part], axis=2).reshape(count, modes * 2 * square)


def self_energy(wannier, vector, energy, vectors, levels, kq_index, omega, phonon):
    matrix = wannier.astype(jnp.float32)

    def fold(x, y):
        return jnp.einsum("wac,cn->wan", x, y, precision=HIGHEST)

    fold_real = fold(matrix[:, 0], vector[0]) - fold(matrix[:, 1], vector[1])
    fold_imag = fold(matrix[:, 0], vector[1]) + fold(matrix[:, 1], vector[0])
    right = jnp.stack(
        [jnp.stack([fold_real, fold_imag]), jnp.stack([fold_imag, -fold_real])], axis=0
    )
    whole = jnp.einsum("kram,rswan->kmswn", vectors, right, precision=HIGHEST)
    points, bands = levels.shape
    table = jnp.concatenate([whole.reshape(points, -1), levels], axis=1)
    hits = (kq_index[:, None] == jnp.arange(points)[None, :]).astype(jnp.float32)
    rows = jnp.dot(hits, table, precision=HIGHEST, preferred_element_type=jnp.float32)
    kq_levels = rows[:, -bands:]
    picked = rows[:, :-bands].reshape((rows.shape[0],) + whole.shape[1:])
    final = jnp.einsum("qmswn,qwv->qsvmn", picked, phonon, precision=HIGHEST)
    strength = final[:, 0] * final[:, 0] + final[:, 1] * final[:, 1]
    fermi = 1.0 / (1.0 + jnp.exp(kq_levels / THERMAL))
    bose = 1.0 / jnp.expm1(omega / THERMAL)
    spacing = energy[None, None, None, :] - kq_levels[:, None, :, None]
    shift = omega[:, :, None, None]
    bose_wide = bose[:, :, None, None]
    fermi_wide = fermi[:, None, :, None]
    occupy = (bose_wide + fermi_wide) * lorentz(spacing + shift) + (
        bose_wide + 1.0 - fermi_wide
    ) * lorentz(spacing - shift)
    return jnp.sum(strength * occupy, axis=(0, 1, 2)) / kq_index.shape[0]


def shards(
    coupling, eigvec, energies, k_coords, r_coords, degeneracy, kq_index, omega, phonon_modes
):
    points, bands = energies.shape
    local_modes = coupling.shape[1]
    square = bands * bands
    groups = lax.axis_size("pb")
    holders = lax.axis_size("ka")
    group = lax.axis_index("pb")
    slab = coupling.reshape(coupling.shape[0], -1)
    partial_value = fourier_terms(k_coords, r_coords, degeneracy, slab, local_modes, square)
    partial_value = partial_value.reshape(holders, -1)
    share = eigvec.reshape(groups, -1)
    share = lax.dynamic_index_in_dim(share, group, 0, keepdims=False)
    extras = [share, energies.reshape(-1), kq_index.astype(jnp.float32).reshape(-1)]
    extras += [omega.reshape(-1), phonon_modes.reshape(-1)]
    sizes = [x.shape[0] for x in extras]
    tail = jnp.concatenate(extras)
    sums = partial_value.shape[1]
    length = -(-(sums + tail.shape[0]) // 128) * 128
    tail = jnp.pad(tail, (0, length - sums - tail.shape[0]))
    parcel = jnp.concatenate(
        [partial_value, jnp.broadcast_to(tail[None], (holders, tail.shape[0]))], axis=1
    )
    parcel = jnp.broadcast_to(parcel[None], (groups, holders, length))
    got = lax.all_to_all(
        parcel.reshape(groups * holders, length // 128, 128), ("pb", "ka"), 0, 0, tiled=True
    ).reshape(groups, holders, length)
    own = lax.axis_index("ka")
    wannier = jnp.sum(got[:, :, :sums], axis=1).astype(jnp.bfloat16)
    wannier = wannier.reshape(groups, points, local_modes, 2, bands, bands)
    fields = []
    start = sums
    for size in sizes:
        fields.append(got[:, :, start : start + size])
        start += size
    all_vectors = jnp.swapaxes(fields[0], 0, 1).reshape(holders * points, 2, bands, bands)
    all_levels = fields[1][0].reshape(holders * points, bands)
    targets = lax.dynamic_index_in_dim(fields[2], own, 1, keepdims=False)
    targets = targets.reshape(groups, points, -1).astype(jnp.int32)
    all_omega = fields[3][:, 0].reshape((-1,) + omega.shape[1:])
    all_phonon = fields[4][:, 0].reshape((-1,) + phonon_modes.shape[1:])
    width = bands // groups
    results = []
    for point in range(points):
        vector = eigvec[point].reshape(2, bands, bands)
        results.append(
            self_energy(
                wannier[:, point].reshape(groups * local_modes, 2, bands, bands),
                lax.dynamic_slice_in_dim(vector, group * width, width, 2),
                lax.dynamic_slice_in_dim(energies[point], group * width, width, 0),
                all_vectors.reshape(-1, 2, bands, bands),
                all_levels,
                targets[:, point].reshape(-1),
                all_omega,
                all_phonon,
            )
        )
    return jnp.stack(results)


def solution(mesh):
    in_specs = (
        P("ka", "pb", None),
        P("ka", None),
        P("ka", None),
        P(),
        P(None, "ka"),
        P("ka"),
        P("ka", "pb"),
        P("pb", None),
        P("pb", None, None),
    )
    out_specs = P("ka", "pb")
    return jax.shard_map(shards, mesh=mesh, in_specs=in_specs, out_specs=out_specs, check_vma=False)
```

```python
import functools
import math

import jax
import jax.numpy as jnp
from jax import lax
from jax.experimental import pallas as pl
from jax.experimental.pallas import tpu as pltpu
from jax.sharding import PartitionSpec as P

KGRID = 64
LANES = 128
HALF = LANES // 2

THERMAL = 0.1
SMEARING = 0.05
HIGHEST = lax.Precision.HIGHEST
F32 = jnp.float32
BF16 = jnp.bfloat16
VMEM = pl.BlockSpec(memory_space=pltpu.VMEM)
SMEM = pl.BlockSpec(memory_space=pltpu.SMEM)


def wave(turns):
    quarter = KGRID // 4
    turn = turns & (KGRID - 1)
    quadrant = (turn + quarter // 2) // quarter
    angle = (turn - quadrant * quarter).astype(F32) * (2.0 * math.pi / KGRID)
    square = angle * angle
    near = 1.0 + square * (
        -1 / 2 + square * (1 / 24 + square * (-1 / 720 + square * (1 / 40320)))
    )
    far = angle * (
        1.0 + square * (-1 / 6 + square * (1 / 120 + square * (-1 / 5040 + square * (1 / 362880))))
    )
    odd = (quadrant & 1) == 1
    cosine = jnp.where(odd, far, near)
    sine = jnp.where(odd, near, far)
    cosine = jnp.where(((quadrant + 1) & 2) == 2, -cosine, cosine)
    sine = jnp.where((quadrant & 2) == 2, -sine, sine)
    return cosine, sine


def pack_kernel(
    groups, place, k_ref, r_ref, degeneracy_ref, coupling_ref, vector_ref, energy_ref,
    index_ref, omega_ref, phonon_ref, out_ref, rows_ref, extra_ref,
):
    count = k_ref.shape[1]
    width = coupling_ref.shape[1]
    tiles = width // LANES
    share = tiles // groups
    turns = lax.dot_general(
        k_ref[...].astype(F32), r_ref[...].astype(F32), (((0,), (0,)), ((), ())),
        preferred_element_type=F32, precision=HIGHEST,
    ).astype(jnp.int32)
    cosine, sine = wave(turns)
    inverse = 1.0 / degeneracy_ref[...].astype(F32)
    both = jnp.concatenate([cosine * inverse, sine * inverse], axis=0).astype(BF16)
    step = 2 * LANES
    for start in range(0, width // 2, step):
        left = jnp.dot(both, coupling_ref[:, start : start + step], preferred_element_type=F32)
        other = start + width // 2
        right = jnp.dot(both, coupling_ref[:, other : other + step], preferred_element_type=F32)
        real = left[:count] - right[count:]
        imag = right[:count] + left[count:]
        for piece in range(step // LANES):
            tile = start // LANES + piece
            lanes = slice(piece * LANES, (piece + 1) * LANES)
            rows_ref[pl.ds(tile, count, tiles), :] = real[:, lanes]
            rows_ref[pl.ds(tile + tiles // 2, count, tiles), :] = imag[:, lanes]
    extra_ref[...] = jnp.zeros_like(extra_ref)
    bands, queries, modes = energy_ref.shape[1], index_ref.shape[1], omega_ref.shape[0]
    extra_ref[0:1, :bands] = energy_ref[...]
    extra_ref[1:2, :queries] = index_ref[...].astype(F32)
    extra_ref[2 : 2 + modes, :queries] = omega_ref[...]
    for mode in range(phonon_ref.shape[0]):
        first = 2 + modes * (1 + mode)
        extra_ref[first : first + modes, :queries] = phonon_ref[mode]
    extra = extra_ref[...]
    high = extra.astype(BF16).astype(F32)
    low = pltpu.roll(extra - high, HALF, 1)
    lane = lax.broadcasted_iota(jnp.int32, extra.shape, 1)
    extra = jnp.where(lane < HALF, high, low)
    mine = vector_ref[0:share, :]
    for group in range(1, groups):
        mine = jnp.where(place[0] == group, vector_ref[group * share : (group + 1) * share, :], mine)
    tail = jnp.concatenate([mine, extra], axis=0).astype(BF16)
    for row in range(count):
        block = rows_ref[row * tiles : (row + 1) * tiles, :].astype(BF16)
        for group in range(groups):
            out_ref[group * count + row, :tiles, :] = block
            out_ref[group * count + row, tiles:, :] = tail


def split(value):
    high = value.astype(BF16)
    return high, (value - high.astype(F32)).astype(BF16)


def energy_kernel(
    groups, bands, queries, place, got_ref, vector_ref, energy_ref, out_ref,
    turned_ref, level_ref, index_ref, scalar_ref, semaphore,
):
    own_group, own_holder = place[0], place[1]
    holders = got_ref.shape[0] // groups
    tiles = 2 * bands * bands // LANES
    share = tiles // groups
    fold = LANES // bands
    half = tiles // 2
    modes = groups
    width = bands // groups
    begin = tiles + share
    for group in range(groups):
        row = got_ref[group * holders + own_holder, begin : begin + 8, :].astype(F32)
        index_ref[group] = row.astype(jnp.int32)
    copy = pltpu.make_async_copy(index_ref, scalar_ref, semaphore)
    copy.start()
    lane = lax.broadcasted_iota(jnp.int32, (8, LANES), 1)
    slot = lane // bands
    stack = []
    for mode in range(modes):
        total = got_ref[mode * holders, :tiles, :].astype(F32)
        for holder in range(1, holders):
            total = total + got_ref[mode * holders + holder, :tiles, :].astype(F32)
        for part in range(2):
            block = total[part * half : (part + 1) * half]
            for piece in range(fold):
                stack.append(block[:, piece * bands : (piece + 1) * bands])
    matrix = jnp.concatenate(stack, axis=0)
    vector = vector_ref[:, :, :width]
    for group in range(1, groups):
        other = vector_ref[:, :, group * width : (group + 1) * width]
        vector = jnp.where(own_group == group, other, vector)
    with_real = jnp.dot(matrix, vector[0], precision=HIGHEST, preferred_element_type=F32)
    with_imag = jnp.dot(matrix, vector[1], precision=HIGHEST, preferred_element_type=F32)
    reals, imags = [], []
    for mode in range(modes):
        top = slice(2 * mode * bands, (2 * mode + 1) * bands)
        low = slice((2 * mode + 1) * bands, (2 * mode + 2) * bands)
        reals.append(with_real[top] - with_imag[low])
        imags.append(with_imag[top] + with_real[low])
    folded = jnp.concatenate(
        [
            jnp.concatenate(reals + imags, axis=1),
            jnp.concatenate(imags + [-x for x in reals], axis=1),
        ],
        axis=0,
    )
    left = folded.T
    left_high, left_low = split(left)
    for holder in range(holders):
        tile = [
            got_ref[group * holders + holder, tiles : tiles + share, :].astype(F32)
            for group in range(groups)
        ]
        tile = jnp.concatenate(tile, axis=0) if groups > 1 else tile[0]
        turned_ref[0, holder] = tile
        for turn in range(1, fold):
            turned_ref[turn, holder] = pltpu.roll(tile, turn * bands, 1)
        row = got_ref[holder, begin : begin + 8, :].astype(F32)
        row = jnp.where(lane < HALF, row + pltpu.roll(row, HALF, 1), 0.0)
        row = jnp.where(slot < 1, row, 0.0)
        full = row
        for turn in range(1, fold):
            full = full + pltpu.roll(row, turn * bands, 1)
        level_ref[holder] = full
    span = queries * bands
    source = lax.broadcasted_iota(jnp.int32, (LANES, span), 0) % HALF
    target = lax.broadcasted_iota(jnp.int32, (LANES, span), 1) // bands
    spread = jnp.where(source == target, 1.0, 0.0).astype(BF16)
    down = lax.broadcasted_iota(jnp.int32, (width, bands), 0) + own_group * width
    across = lax.broadcasted_iota(jnp.int32, (width, bands), 1)
    energy = jnp.sum(jnp.where(down == across, energy_ref[...], 0.0), axis=1, keepdims=True)
    copy.wait()
    total = jnp.zeros((width, LANES), F32)
    for group in range(groups):
        table = jnp.dot(
            got_ref[group * holders, begin:, :], spread, preferred_element_type=F32
        )
        for start in range(0, queries, fold):
            points = [scalar_ref[group, 1, start + item] for item in range(fold)]
            level = level_ref[points[0]]
            for item in range(1, fold):
                level = jnp.where(slot == item, level_ref[points[item]], level)
            level = level[0:1]
            blocks = []
            for part in range(2):
                for piece in range(fold):
                    rows = slice(part * half, (part + 1) * half)
                    block = turned_ref[(-piece) % fold, points[0], rows, :]
                    for item in range(1, fold):
                        block = jnp.where(
                            slot[:half] == item,
                            turned_ref[(item - piece) % fold, points[item], rows, :],
                            block,
                        )
                    blocks.append(block)
            chosen = jnp.concatenate(blocks, axis=0).astype(BF16)
            whole = jnp.dot(left_high, chosen, preferred_element_type=F32) + jnp.dot(
                left_low, chosen, preferred_element_type=F32
            )
            values = table[:, start * bands : (start + fold) * bands]
            fermi = 1.0 / (1.0 + jnp.exp(level / THERMAL))
            spacing = energy - level
            for out_mode in range(modes):
                real = imag = None
                for mode in range(modes):
                    row = 2 + modes * (1 + mode) + out_mode
                    weight = values[row : row + 1]
                    one = whole[mode * width : (mode + 1) * width] * weight
                    two = whole[(modes + mode) * width : (modes + mode + 1) * width] * weight
                    real = one if real is None else real + one
                    imag = two if imag is None else imag + two
                omega = values[2 + out_mode : 3 + out_mode]
                bose = 1.0 / (jnp.exp(omega / THERMAL) - 1.0)
                scale = SMEARING / math.pi
                up = spacing + omega
                off = spacing - omega
                up = up * up + SMEARING * SMEARING
                off = off * off + SMEARING * SMEARING
                absorb = (bose + fermi) * scale
                emit = (bose + 1.0 - fermi) * scale
                total = total + (real * real + imag * imag) * (absorb / up + emit / off)
    total = jnp.sum(total.T, axis=0, keepdims=True)
    out_ref[...] = total * (1.0 / (groups * queries))


def shards(
    coupling, eigvec, energies, k_coords, r_coords, degeneracy, kq_index, omega, phonon_modes
):
    groups = lax.axis_size("pb")
    holders = lax.axis_size("ka")
    bands = energies.shape[1]
    queries = kq_index.shape[1]
    modes = omega.shape[1]
    slab = coupling.reshape(coupling.shape[0], -1)
    tiles = slab.shape[1] // LANES
    place = jnp.stack([lax.axis_index("pb"), lax.axis_index("ka")])
    share = tiles // groups
    extra = -(-(share + 2 + modes * (modes + 1)) // 16) * 16 - share
    length = tiles + share + extra
    parcel = pl.pallas_call(
        functools.partial(pack_kernel, groups),
        out_shape=jax.ShapeDtypeStruct((groups * holders, length, LANES), BF16),
        in_specs=[SMEM] + [VMEM] * 9,
        out_specs=VMEM,
        scratch_shapes=[
            pltpu.VMEM((holders * tiles, LANES), F32),
            pltpu.VMEM((extra, LANES), F32),
        ],
        name="pack",
    )(
        place, k_coords, r_coords, degeneracy.reshape(1, -1), slab, eigvec.reshape(tiles, LANES),
        energies, kq_index, omega.T, phonon_modes.transpose(1, 2, 0),
    )
    got = lax.all_to_all(parcel, ("pb", "ka"), 0, 0, tiled=True)
    return pl.pallas_call(
        functools.partial(energy_kernel, groups, bands, queries),
        out_shape=jax.ShapeDtypeStruct((1, bands // groups), F32),
        in_specs=[SMEM] + [VMEM] * 3,
        out_specs=VMEM,
        scratch_shapes=[
            pltpu.VMEM((LANES // bands, holders, tiles, LANES), F32),
            pltpu.VMEM((holders, 8, LANES), F32),
            pltpu.VMEM((groups, 8, LANES), jnp.int32),
            pltpu.SMEM((groups, 8, LANES), jnp.int32),
            pltpu.SemaphoreType.DMA,
        ],
        name="energy",
    )(place, got, eigvec.reshape(2, bands, bands), energies)


def solution(mesh):
    in_specs = (
        P("ka", "pb", None),
        P("ka", None),
        P("ka", None),
        P(),
        P(None, "ka"),
        P("ka"),
        P("ka", "pb"),
        P("pb", None),
        P("pb", None, None),
    )
    out_specs = P("ka", "pb")
    return jax.shard_map(shards, mesh=mesh, in_specs=in_specs, out_specs=out_specs, check_vma=False)
```

```python
import functools
import math

import jax
import jax.numpy as jnp
from jax import lax
from jax.experimental import pallas as pl
from jax.experimental.pallas import tpu as pltpu
from jax.sharding import PartitionSpec as P

KGRID = 64
LANES = 128
HALF = LANES // 2

THERMAL = 0.1
SMEARING = 0.05
HIGHEST = lax.Precision.HIGHEST
F32 = jnp.float32
BF16 = jnp.bfloat16
VMEM = pl.BlockSpec(memory_space=pltpu.VMEM)


def wave(turns):
    quarter = KGRID // 4
    turn = turns & (KGRID - 1)
    quadrant = (turn + quarter // 2) // quarter
    angle = (turn - quadrant * quarter).astype(F32) * (2.0 * math.pi / KGRID)
    square = angle * angle
    near = 1.0 + square * (
        -1 / 2 + square * (1 / 24 + square * (-1 / 720 + square * (1 / 40320)))
    )
    far = angle * (
        1.0 + square * (-1 / 6 + square * (1 / 120 + square * (-1 / 5040 + square * (1 / 362880))))
    )
    odd = (quadrant & 1) == 1
    cosine = jnp.where(odd, far, near)
    sine = jnp.where(odd, near, far)
    cosine = jnp.where(((quadrant + 1) & 2) == 2, -cosine, cosine)
    sine = jnp.where((quadrant & 2) == 2, -sine, sine)
    return cosine, sine


def pack_kernel(
    groups, k_ref, r_ref, degeneracy_ref, coupling_ref, vector_ref, energy_ref,
    index_ref, omega_ref, phonon_ref, out_ref, rows_ref, extra_ref,
):
    place = lax.axis_index("pb")
    count = k_ref.shape[1]
    width = coupling_ref.shape[1]
    tiles = width // LANES
    share = tiles // groups
    turns = lax.dot_general(
        k_ref[...].astype(F32), r_ref[...].astype(F32), (((0,), (0,)), ((), ())),
        preferred_element_type=F32, precision=HIGHEST,
    ).astype(jnp.int32)
    cosine, sine = wave(turns)
    inverse = 1.0 / degeneracy_ref[...].astype(F32).reshape(1, -1)
    both = jnp.concatenate([cosine * inverse, sine * inverse], axis=0).astype(BF16)
    step = 2 * LANES
    for start in range(0, width // 2, step):
        left = jnp.dot(both, coupling_ref[:, start : start + step], preferred_element_type=F32)
        other = start + width // 2
        right = jnp.dot(both, coupling_ref[:, other : other + step], preferred_element_type=F32)
        real = left[:count] - right[count:]
        imag = right[:count] + left[count:]
        for piece in range(step // LANES):
            tile = start // LANES + piece
            lanes = slice(piece * LANES, (piece + 1) * LANES)
            rows_ref[pl.ds(tile, count, tiles), :] = real[:, lanes]
            rows_ref[pl.ds(tile + tiles // 2, count, tiles), :] = imag[:, lanes]
    extra_ref[...] = jnp.zeros_like(extra_ref)
    bands, queries, modes = energy_ref.shape[1], index_ref.shape[1], omega_ref.shape[0]
    extra_ref[0:1, :bands] = energy_ref[...]
    extra_ref[1:2, :queries] = index_ref[...].astype(F32)
    extra_ref[2 : 2 + modes, :queries] = omega_ref[...]
    for mode in range(phonon_ref.shape[0]):
        first = 2 + modes * (1 + mode)
        extra_ref[first : first + modes, :queries] = phonon_ref[mode]
    extra = extra_ref[...]
    high = extra.astype(BF16).astype(F32)
    low = pltpu.roll(extra - high, HALF, 1)
    lane = lax.broadcasted_iota(jnp.int32, extra.shape, 1)
    extra = jnp.where(lane < HALF, high, low)
    mine = vector_ref[0:share, :]
    for group in range(1, groups):
        mine = jnp.where(place == group, vector_ref[group * share : (group + 1) * share, :], mine)
    tail = jnp.concatenate([mine, extra], axis=0).astype(BF16)
    for row in range(count):
        block = rows_ref[row * tiles : (row + 1) * tiles, :].astype(BF16)
        for group in range(groups):
            out_ref[group * count + row, :tiles, :] = block
            out_ref[group * count + row, tiles:, :] = tail


def split(value):
    high = value.astype(BF16)
    return high, (value - high.astype(F32)).astype(BF16)


def energy_kernel(
    groups, bands, queries, got_ref, vector_ref, energy_ref, out_ref,
    turned_ref, level_ref, index_ref, scalar_ref, semaphore,
):
    own_group, own_holder = lax.axis_index("pb"), lax.axis_index("ka")
    holders = got_ref.shape[0] // groups
    tiles = 2 * bands * bands // LANES
    share = tiles // groups
    fold = LANES // bands
    half = tiles // 2
    modes = groups
    width = bands // groups
    begin = tiles + share
    for group in range(groups):
        row = got_ref[group * holders + own_holder, begin : begin + 8, :].astype(F32)
        index_ref[group] = row.astype(jnp.int32)
    copy = pltpu.make_async_copy(index_ref, scalar_ref, semaphore)
    copy.start()
    lane = lax.broadcasted_iota(jnp.int32, (8, LANES), 1)
    slot = lane // bands
    stack = []
    for mode in range(modes):
        total = got_ref[mode * holders, :tiles, :].astype(F32)
        for holder in range(1, holders):
            total = total + got_ref[mode * holders + holder, :tiles, :].astype(F32)
        for part in range(2):
            block = total[part * half : (part + 1) * half]
            for piece in range(fold):
                stack.append(block[:, piece * bands : (piece + 1) * bands])
    matrix = jnp.concatenate(stack, axis=0)
    vector = vector_ref[:, :, :width]
    for group in range(1, groups):
        other = vector_ref[:, :, group * width : (group + 1) * width]
        vector = jnp.where(own_group == group, other, vector)
    with_real = jnp.dot(matrix, vector[0], precision=HIGHEST, preferred_element_type=F32)
    with_imag = jnp.dot(matrix, vector[1], precision=HIGHEST, preferred_element_type=F32)
    reals, imags = [], []
    for mode in range(modes):
        top = slice(2 * mode * bands, (2 * mode + 1) * bands)
        low = slice((2 * mode + 1) * bands, (2 * mode + 2) * bands)
        reals.append(with_real[top] - with_imag[low])
        imags.append(with_imag[top] + with_real[low])
    folded = jnp.concatenate(
        [
            jnp.concatenate(reals + imags, axis=1),
            jnp.concatenate(imags + [-x for x in reals], axis=1),
        ],
        axis=0,
    )
    left = folded.T
    left_high, left_low = split(left)
    for holder in range(holders):
        tile = [
            got_ref[group * holders + holder, tiles : tiles + share, :].astype(F32)
            for group in range(groups)
        ]
        tile = jnp.concatenate(tile, axis=0) if groups > 1 else tile[0]
        turned_ref[0, holder] = tile
        for turn in range(1, fold):
            turned_ref[turn, holder] = pltpu.roll(tile, turn * bands, 1)
        row = got_ref[holder, begin : begin + 8, :].astype(F32)
        row = jnp.where(lane < HALF, row + pltpu.roll(row, HALF, 1), 0.0)
        row = jnp.where(slot < 1, row, 0.0)
        full = row
        for turn in range(1, fold):
            full = full + pltpu.roll(row, turn * bands, 1)
        level_ref[holder] = full
    span = queries * bands
    source = lax.broadcasted_iota(jnp.int32, (LANES, span), 0) % HALF
    target = lax.broadcasted_iota(jnp.int32, (LANES, span), 1) // bands
    spread = jnp.where(source == target, 1.0, 0.0).astype(BF16)
    down = lax.broadcasted_iota(jnp.int32, (width, bands), 0) + own_group * width
    across = lax.broadcasted_iota(jnp.int32, (width, bands), 1)
    energy = jnp.sum(jnp.where(down == across, energy_ref[...], 0.0), axis=1, keepdims=True)
    copy.wait()
    total = jnp.zeros((width, LANES), F32)
    for group in range(groups):
        table = jnp.dot(
            got_ref[group * holders, begin:, :], spread, preferred_element_type=F32
        )
        for start in range(0, queries, fold):
            points = [scalar_ref[group, 1, start + item] for item in range(fold)]
            level = level_ref[points[0]]
            for item in range(1, fold):
                level = jnp.where(slot == item, level_ref[points[item]], level)
            level = level[0:1]
            blocks = []
            for part in range(2):
                for piece in range(fold):
                    rows = slice(part * half, (part + 1) * half)
                    block = turned_ref[(-piece) % fold, points[0], rows, :]
                    for item in range(1, fold):
                        block = jnp.where(
                            slot[:half] == item,
                            turned_ref[(item - piece) % fold, points[item], rows, :],
                            block,
                        )
                    blocks.append(block)
            chosen = jnp.concatenate(blocks, axis=0).astype(BF16)
            whole = jnp.dot(left_high, chosen, preferred_element_type=F32) + jnp.dot(
                left_low, chosen, preferred_element_type=F32
            )
            values = table[:, start * bands : (start + fold) * bands]
            fermi = 1.0 / (1.0 + jnp.exp(level / THERMAL))
            spacing = energy - level
            for out_mode in range(modes):
                real = imag = None
                for mode in range(modes):
                    row = 2 + modes * (1 + mode) + out_mode
                    weight = values[row : row + 1]
                    one = whole[mode * width : (mode + 1) * width] * weight
                    two = whole[(modes + mode) * width : (modes + mode + 1) * width] * weight
                    real = one if real is None else real + one
                    imag = two if imag is None else imag + two
                omega = values[2 + out_mode : 3 + out_mode]
                bose = 1.0 / (jnp.exp(omega / THERMAL) - 1.0)
                scale = SMEARING / math.pi
                up = spacing + omega
                off = spacing - omega
                up = up * up + SMEARING * SMEARING
                off = off * off + SMEARING * SMEARING
                absorb = (bose + fermi) * scale
                emit = (bose + 1.0 - fermi) * scale
                total = total + (real * real + imag * imag) * (absorb / up + emit / off)
    total = jnp.sum(total.T, axis=0, keepdims=True)
    out_ref[...] = total * (1.0 / (groups * queries))


def grant(size):
    return size + size // 4 + (2 << 20)


def shards(
    coupling, eigvec, energies, k_coords, r_coords, degeneracy, kq_index, omega, phonon_modes
):
    groups = lax.axis_size("pb")
    holders = lax.axis_size("ka")
    bands = energies.shape[1]
    queries = kq_index.shape[1]
    modes = omega.shape[1]
    slab = coupling.reshape(coupling.shape[0], -1)
    tiles = slab.shape[1] // LANES
    share = tiles // groups
    extra = -(-(share + 2 + modes * (modes + 1)) // 16) * 16 - share
    length = tiles + share + extra
    parcel = pl.pallas_call(
        functools.partial(pack_kernel, groups),
        out_shape=jax.ShapeDtypeStruct((groups * holders, length, LANES), BF16),
        in_specs=[VMEM] * 9,
        out_specs=VMEM,
        scratch_shapes=[
            pltpu.VMEM((holders * tiles, LANES), F32),
            pltpu.VMEM((extra, LANES), F32),
        ],
        name="pack",
    )(
        k_coords, r_coords, degeneracy, slab, eigvec.reshape(tiles, LANES),
        energies, kq_index, omega.T, phonon_modes.transpose(1, 2, 0),
    )
    got = lax.all_to_all(parcel, ("pb", "ka"), 0, 0, tiled=True)
    return pl.pallas_call(
        functools.partial(energy_kernel, groups, bands, queries),
        out_shape=jax.ShapeDtypeStruct((1, bands // groups), F32),
        in_specs=[VMEM] * 3,
        out_specs=VMEM,
        scratch_shapes=[
            pltpu.VMEM((LANES // bands, holders, tiles, LANES), F32),
            pltpu.VMEM((holders, 8, LANES), F32),
            pltpu.VMEM((groups, 8, LANES), jnp.int32),
            pltpu.SMEM((groups, 8, LANES), jnp.int32),
            pltpu.SemaphoreType.DMA,
        ],
        compiler_params=pltpu.CompilerParams(
            vmem_limit_bytes=grant(
                2 * got.size + 4 * LANES * holders * (tiles * LANES // bands + 8)
            )
        ),
        name="energy",
    )(got, eigvec.reshape(2, bands, bands), energies)


def solution(mesh):
    in_specs = (
        P("ka", "pb", None),
        P("ka", None),
        P("ka", None),
        P(),
        P(None, "ka"),
        P("ka"),
        P("ka", "pb"),
        P("pb", None),
        P("pb", None, None),
    )
    out_specs = P("ka", "pb")
    return jax.shard_map(shards, mesh=mesh, in_specs=in_specs, out_specs=out_specs, check_vma=False)
```

```python
import functools
import math

import jax
import jax.numpy as jnp
from jax import lax
from jax.experimental import pallas as pl
from jax.experimental.pallas import tpu as pltpu
from jax.sharding import PartitionSpec as P

KGRID = 64
LANES = 128
HALF = LANES // 2
CHUNKS = 4

THERMAL = 0.1
SMEARING = 0.05
HIGHEST = lax.Precision.HIGHEST
F32 = jnp.float32
BF16 = jnp.bfloat16
HBM = pl.BlockSpec(memory_space=pltpu.HBM)
VMEM = pl.BlockSpec(memory_space=pltpu.VMEM)


def wave(turns):
    quarter = KGRID // 4
    turn = turns & (KGRID - 1)
    quadrant = (turn + quarter // 2) // quarter
    angle = (turn - quadrant * quarter).astype(F32) * (2.0 * math.pi / KGRID)
    square = angle * angle
    near = 1.0 + square * (
        -1 / 2 + square * (1 / 24 + square * (-1 / 720 + square * (1 / 40320)))
    )
    far = angle * (
        1.0 + square * (-1 / 6 + square * (1 / 120 + square * (-1 / 5040 + square * (1 / 362880))))
    )
    odd = (quadrant & 1) == 1
    cosine = jnp.where(odd, far, near)
    sine = jnp.where(odd, near, far)
    cosine = jnp.where(((quadrant + 1) & 2) == 2, -cosine, cosine)
    sine = jnp.where((quadrant & 2) == 2, -sine, sine)
    return cosine, sine


def pack_kernel(
    groups, k_ref, r_ref, degeneracy_ref, coupling_ref, vector_ref, energy_ref,
    index_ref, omega_ref, phonon_ref, out_ref, rows_ref, extra_ref,
):
    place = lax.axis_index("pb")
    count = k_ref.shape[1]
    width = coupling_ref.shape[1]
    tiles = width // LANES
    share = tiles // groups
    turns = lax.dot_general(
        k_ref[...].astype(F32), r_ref[...].astype(F32), (((0,), (0,)), ((), ())),
        preferred_element_type=F32, precision=HIGHEST,
    ).astype(jnp.int32)
    cosine, sine = wave(turns)
    inverse = 1.0 / degeneracy_ref[...].astype(F32).reshape(1, -1)
    both = jnp.concatenate([cosine * inverse, sine * inverse], axis=0).astype(BF16)
    extra_ref[...] = jnp.zeros_like(extra_ref)
    bands, queries, modes = energy_ref.shape[1], index_ref.shape[1], omega_ref.shape[0]
    extra_ref[0:1, :bands] = energy_ref[...]
    extra_ref[1:2, :queries] = index_ref[...].astype(F32)
    extra_ref[2 : 2 + modes, :queries] = omega_ref[...]
    for mode in range(phonon_ref.shape[0]):
        first = 2 + modes * (1 + mode)
        extra_ref[first : first + modes, :queries] = phonon_ref[mode]
    extra = extra_ref[...]
    high = extra.astype(BF16).astype(F32)
    low = pltpu.roll(extra - high, HALF, 1)
    lane = lax.broadcasted_iota(jnp.int32, extra.shape, 1)
    extra = jnp.where(lane < HALF, high, low)
    mine = vector_ref[0:share, :]
    for group in range(1, groups):
        mine = jnp.where(place == group, vector_ref[group * share : (group + 1) * share, :], mine)
    tail = jnp.concatenate([mine, extra], axis=0).astype(BF16)
    step = 2 * LANES
    for start in range(0, width // 2, step):
        left = jnp.dot(both, coupling_ref[:, start : start + step], preferred_element_type=F32)
        other = start + width // 2
        right = jnp.dot(both, coupling_ref[:, other : other + step], preferred_element_type=F32)
        real = left[:count] - right[count:]
        imag = right[:count] + left[count:]
        for piece in range(step // LANES):
            tile = start // LANES + piece
            lanes = slice(piece * LANES, (piece + 1) * LANES)
            rows_ref[pl.ds(tile, count, tiles), :] = real[:, lanes]
            rows_ref[pl.ds(tile + tiles // 2, count, tiles), :] = imag[:, lanes]
    for row in range(count):
        block = rows_ref[row * tiles : (row + 1) * tiles, :].astype(BF16)
        for group in range(groups):
            out_ref[group * count + row, :tiles, :] = block
            out_ref[group * count + row, tiles:, :] = tail


def split(value):
    high = value.astype(BF16)
    return high, (value - high.astype(F32)).astype(BF16)


def energy_kernel(
    groups, bands, queries, got_ref, vector_ref, energy_ref, out_ref,
    turned_ref, level_ref, flat_ref, index_ref, scalar_ref, semaphore,
):
    own_group, own_holder = lax.axis_index("pb"), lax.axis_index("ka")
    holders = got_ref.shape[0] // groups
    tiles = 2 * bands * bands // LANES
    share = tiles // groups
    fold = LANES // bands
    half = tiles // 2
    modes = groups
    width = bands // groups
    begin = tiles + share
    for group in range(groups):
        row = got_ref[group * holders + own_holder, begin : begin + 8, :].astype(F32)
        index_ref[group] = row.astype(jnp.int32)
    copy = pltpu.make_async_copy(index_ref, scalar_ref, semaphore)
    copy.start()
    lane = lax.broadcasted_iota(jnp.int32, (8, LANES), 1)
    slot = lane // bands
    stack = []
    for mode in range(modes):
        total = got_ref[mode * holders, :tiles, :].astype(F32)
        for holder in range(1, holders):
            total = total + got_ref[mode * holders + holder, :tiles, :].astype(F32)
        for part in range(2):
            block = total[part * half : (part + 1) * half]
            for piece in range(fold):
                stack.append(block[:, piece * bands : (piece + 1) * bands])
    matrix = jnp.concatenate(stack, axis=0)
    vector = []
    for part in range(2):
        block = vector_ref[part * half : (part + 1) * half, :]
        for piece in range(fold):
            first = piece * bands
            value = block[:, first : first + width]
            for group in range(1, groups):
                other = block[:, first + group * width : first + (group + 1) * width]
                value = jnp.where(own_group == group, other, value)
            flat_ref[part, pl.ds(piece, half, fold), :width] = value
        vector.append(flat_ref[part, :, :width])
    with_real = jnp.dot(matrix, vector[0], precision=HIGHEST, preferred_element_type=F32)
    with_imag = jnp.dot(matrix, vector[1], precision=HIGHEST, preferred_element_type=F32)
    reals, imags = [], []
    for mode in range(modes):
        top = slice(2 * mode * bands, (2 * mode + 1) * bands)
        low = slice((2 * mode + 1) * bands, (2 * mode + 2) * bands)
        reals.append(with_real[top] - with_imag[low])
        imags.append(with_imag[top] + with_real[low])
    folded = jnp.concatenate(
        [
            jnp.concatenate(reals + imags, axis=1),
            jnp.concatenate(imags + [-x for x in reals], axis=1),
        ],
        axis=0,
    )
    left = folded.T
    left_high, left_low = split(left)
    for holder in range(holders):
        tile = [
            got_ref[group * holders + holder, tiles : tiles + share, :].astype(F32)
            for group in range(groups)
        ]
        tile = jnp.concatenate(tile, axis=0) if groups > 1 else tile[0]
        turned_ref[0, holder] = tile
        for turn in range(1, fold):
            turned_ref[turn, holder] = pltpu.roll(tile, turn * bands, 1)
        row = got_ref[holder, begin : begin + 8, :].astype(F32)
        row = jnp.where(lane < HALF, row + pltpu.roll(row, HALF, 1), 0.0)
        row = jnp.where(slot < 1, row, 0.0)
        full = row
        for turn in range(1, fold):
            full = full + pltpu.roll(row, turn * bands, 1)
        level_ref[holder] = full
    span = queries * bands
    source = lax.broadcasted_iota(jnp.int32, (LANES, span), 0) % HALF
    target = lax.broadcasted_iota(jnp.int32, (LANES, span), 1) // bands
    spread = jnp.where(source == target, 1.0, 0.0).astype(BF16)
    down = lax.broadcasted_iota(jnp.int32, (width, bands), 0) + own_group * width
    across = lax.broadcasted_iota(jnp.int32, (width, bands), 1)
    energy = jnp.sum(jnp.where(down == across, energy_ref[...], 0.0), axis=1, keepdims=True)
    copy.wait()
    total = jnp.zeros((width, LANES), F32)
    for group in range(groups):
        table = jnp.dot(
            got_ref[group * holders, begin:, :], spread, preferred_element_type=F32
        )
        for start in range(0, queries, fold):
            points = [scalar_ref[group, 1, start + item] for item in range(fold)]
            level = level_ref[points[0]]
            for item in range(1, fold):
                level = jnp.where(slot == item, level_ref[points[item]], level)
            level = level[0:1]
            blocks = []
            for part in range(2):
                for piece in range(fold):
                    rows = slice(part * half, (part + 1) * half)
                    block = turned_ref[(-piece) % fold, points[0], rows, :]
                    for item in range(1, fold):
                        block = jnp.where(
                            slot[:half] == item,
                            turned_ref[(item - piece) % fold, points[item], rows, :],
                            block,
                        )
                    blocks.append(block)
            chosen = jnp.concatenate(blocks, axis=0).astype(BF16)
            whole = jnp.dot(left_high, chosen, preferred_element_type=F32) + jnp.dot(
                left_low, chosen, preferred_element_type=F32
            )
            values = table[:, start * bands : (start + fold) * bands]
            fermi = 1.0 / (1.0 + jnp.exp(level / THERMAL))
            spacing = energy - level
            for out_mode in range(modes):
                real = imag = None
                for mode in range(modes):
                    row = 2 + modes * (1 + mode) + out_mode
                    weight = values[row : row + 1]
                    one = whole[mode * width : (mode + 1) * width] * weight
                    two = whole[(modes + mode) * width : (modes + mode + 1) * width] * weight
                    real = one if real is None else real + one
                    imag = two if imag is None else imag + two
                omega = values[2 + out_mode : 3 + out_mode]
                bose = 1.0 / (jnp.exp(omega / THERMAL) - 1.0)
                scale = SMEARING / math.pi
                up = spacing + omega
                off = spacing - omega
                up = up * up + SMEARING * SMEARING
                off = off * off + SMEARING * SMEARING
                absorb = (bose + fermi) * scale
                emit = (bose + 1.0 - fermi) * scale
                total = total + (real * real + imag * imag) * (absorb / up + emit / off)
    total = jnp.sum(total.T, axis=0, keepdims=True)
    out_ref[...] = total * (1.0 / (groups * queries))


def grant(size):
    return size + size // 4 + (2 << 20)


def shards(
    coupling, eigvec, energies, k_coords, r_coords, degeneracy, kq_index, omega, phonon_modes
):
    groups = lax.axis_size("pb")
    holders = lax.axis_size("ka")
    bands = energies.shape[1]
    queries = kq_index.shape[1]
    modes = omega.shape[1]
    slab = coupling.reshape(coupling.shape[0], -1)
    tiles = slab.shape[1] // LANES
    share = tiles // groups
    extra = -(-(share + 2 + modes * (modes + 1)) // 16) * 16 - share
    length = tiles + share + extra
    operands = (
        k_coords, r_coords, degeneracy, slab, eigvec.reshape(tiles, LANES),
        energies, kq_index, omega.T, phonon_modes.transpose(1, 2, 0),
    )
    operands = tuple(pltpu.with_memory_space_constraint(x, pltpu.HBM) for x in operands)
    parcel = pl.pallas_call(
        functools.partial(pack_kernel, groups),
        out_shape=jax.ShapeDtypeStruct((groups * holders, length, LANES), BF16),
        in_specs=[VMEM] * 9,
        out_specs=VMEM,
        scratch_shapes=[
            pltpu.VMEM((holders * tiles, LANES), F32),
            pltpu.VMEM((extra, LANES), F32),
        ],
        compiler_params=pltpu.CompilerParams(
            vmem_limit_bytes=grant(2 * (slab.size + groups * holders * length * LANES))
            + 4 * holders * tiles * LANES
        ),
        name="pack",
    )(*operands)
    got = lax.all_to_all(parcel, ("pb", "ka"), 0, 0, tiled=True)
    return pl.pallas_call(
        functools.partial(energy_kernel, groups, bands, queries),
        out_shape=jax.ShapeDtypeStruct((1, bands // groups), F32),
        in_specs=[VMEM] * 3,
        out_specs=VMEM,
        scratch_shapes=[
            pltpu.VMEM((LANES // bands, holders, tiles, LANES), F32),
            pltpu.VMEM((holders, 8, LANES), F32),
            pltpu.VMEM((2, bands, LANES), F32),
            pltpu.VMEM((groups, 8, LANES), jnp.int32),
            pltpu.SMEM((groups, 8, LANES), jnp.int32),
            pltpu.SemaphoreType.DMA,
        ],
        compiler_params=pltpu.CompilerParams(
            vmem_limit_bytes=grant(
                2 * got.size + 4 * LANES * holders * (tiles * LANES // bands + 8)
            )
        ),
        name="energy",
    )(got, eigvec.reshape(tiles, LANES), energies)


def solution(mesh):
    in_specs = (
        P("ka", "pb", None),
        P("ka", None),
        P("ka", None),
        P(),
        P(None, "ka"),
        P("ka"),
        P("ka", "pb"),
        P("pb", None),
        P("pb", None, None),
    )
    out_specs = P("ka", "pb")
    return jax.shard_map(shards, mesh=mesh, in_specs=in_specs, out_specs=out_specs, check_vma=False)
```

```python
import functools
import math

import jax
import jax.numpy as jnp
from jax import lax
from jax.experimental import pallas as pl
from jax.experimental.pallas import tpu as pltpu
from jax.sharding import PartitionSpec as P

KGRID = 64
LANES = 128
HALF = LANES // 2
CHUNKS = 4

THERMAL = 0.1
SMEARING = 0.05
HIGHEST = lax.Precision.HIGHEST
F32 = jnp.float32
BF16 = jnp.bfloat16
HBM = pl.BlockSpec(memory_space=pltpu.HBM)
VMEM = pl.BlockSpec(memory_space=pltpu.VMEM)


def wave(turns):
    quarter = KGRID // 4
    turn = turns & (KGRID - 1)
    quadrant = (turn + quarter // 2) // quarter
    angle = (turn - quadrant * quarter).astype(F32) * (2.0 * math.pi / KGRID)
    square = angle * angle
    near = 1.0 + square * (
        -1 / 2 + square * (1 / 24 + square * (-1 / 720 + square * (1 / 40320)))
    )
    far = angle * (
        1.0 + square * (-1 / 6 + square * (1 / 120 + square * (-1 / 5040 + square * (1 / 362880))))
    )
    odd = (quadrant & 1) == 1
    cosine = jnp.where(odd, far, near)
    sine = jnp.where(odd, near, far)
    cosine = jnp.where(((quadrant + 1) & 2) == 2, -cosine, cosine)
    sine = jnp.where((quadrant & 2) == 2, -sine, sine)
    return cosine, sine


def pack_kernel(groups, *refs):
    sources, out_ref, (rows_ref, extra_ref) = refs[:9], refs[9], refs[10:12]
    copies, semaphores = refs[12:21], refs[21]
    k_ref, r_ref, degeneracy_ref, coupling_ref, vector_ref, energy_ref = copies[:6]
    index_ref, omega_ref, phonon_ref = copies[6:]
    pending = [
        pltpu.make_async_copy(source, target, semaphores.at[number])
        for number, (source, target) in enumerate(zip(sources, copies, strict=True))
    ]
    slab_copy = pending.pop(3)
    for copy in pending[:3]:
        copy.start()
    slab_copy.start()
    for copy in pending[3:]:
        copy.start()
    for copy in pending:
        copy.wait()
    place = lax.axis_index("pb")
    count = k_ref.shape[1]
    width = coupling_ref.shape[1]
    tiles = width // LANES
    share = tiles // groups
    turns = lax.dot_general(
        k_ref[...].astype(F32).astype(BF16), r_ref[...].astype(F32).astype(BF16),
        (((0,), (0,)), ((), ())), preferred_element_type=F32,
    ).astype(jnp.int32)
    cosine, sine = wave(turns)
    inverse = 1.0 / degeneracy_ref[...].astype(F32).reshape(1, -1)
    both = jnp.concatenate([cosine * inverse, sine * inverse], axis=0).astype(BF16)
    extra_ref[...] = jnp.zeros_like(extra_ref)
    bands, queries, modes = energy_ref.shape[1], index_ref.shape[1], omega_ref.shape[0]
    extra_ref[0:1, :bands] = energy_ref[...]
    extra_ref[1:2, :queries] = index_ref[...].astype(F32)
    extra_ref[2 : 2 + modes, :queries] = omega_ref[...]
    for mode in range(phonon_ref.shape[0]):
        first = 2 + modes * (1 + mode)
        extra_ref[first : first + modes, :queries] = phonon_ref[mode]
    extra = extra_ref[...]
    high = extra.astype(BF16).astype(F32)
    low = pltpu.roll(extra - high, HALF, 1)
    lane = lax.broadcasted_iota(jnp.int32, extra.shape, 1)
    extra = jnp.where(lane < HALF, high, low)
    mine = vector_ref[0:share, :]
    for group in range(1, groups):
        mine = jnp.where(place == group, vector_ref[group * share : (group + 1) * share, :], mine)
    tail = jnp.concatenate([mine, extra], axis=0).astype(BF16)
    slab_copy.wait()
    step = 2 * LANES
    for start in range(0, width // 2, step):
        left = jnp.dot(both, coupling_ref[:, start : start + step], preferred_element_type=F32)
        other = start + width // 2
        right = jnp.dot(both, coupling_ref[:, other : other + step], preferred_element_type=F32)
        real = left[:count] - right[count:]
        imag = right[:count] + left[count:]
        for piece in range(step // LANES):
            tile = start // LANES + piece
            lanes = slice(piece * LANES, (piece + 1) * LANES)
            rows_ref[pl.ds(tile, count, tiles), :] = real[:, lanes]
            rows_ref[pl.ds(tile + tiles // 2, count, tiles), :] = imag[:, lanes]
    for row in range(count):
        block = rows_ref[row * tiles : (row + 1) * tiles, :].astype(BF16)
        for group in range(groups):
            out_ref[group * count + row, :tiles, :] = block
            out_ref[group * count + row, tiles:, :] = tail


def split(value):
    high = value.astype(BF16)
    return high, (value - high.astype(F32)).astype(BF16)


def energy_kernel(
    groups, bands, queries, got_ref, vector_ref, energy_ref, out_ref,
    turned_ref, level_ref, flat_ref, index_ref, scalar_ref, semaphore,
):
    own_group, own_holder = lax.axis_index("pb"), lax.axis_index("ka")
    holders = got_ref.shape[0] // groups
    tiles = 2 * bands * bands // LANES
    share = tiles // groups
    fold = LANES // bands
    half = tiles // 2
    modes = groups
    width = bands // groups
    begin = tiles + share
    copy = pltpu.make_async_copy(index_ref, scalar_ref, semaphore)

    @pl.when(own_holder >= 0)
    def _():
        for group in range(groups):
            row = got_ref[group * holders + own_holder, begin : begin + 8, :].astype(F32)
            index_ref[group] = row.astype(jnp.int32)
        copy.start()

    lane = lax.broadcasted_iota(jnp.int32, (8, LANES), 1)
    slot = lane // bands
    vector = []
    for part in range(2):
        block = vector_ref[part * half : (part + 1) * half, :]
        for piece in range(fold):
            first = piece * bands
            value = block[:, first : first + width]
            for group in range(1, groups):
                other = block[:, first + group * width : first + (group + 1) * width]
                value = jnp.where(own_group == group, other, value)
            flat_ref[part, pl.ds(piece, half, fold), :width] = value
        vector.append(flat_ref[part, :, :width].T)
    vector_high, vector_low = split(jnp.concatenate(vector, axis=0))
    stack = [[], []]
    for mode in range(modes):
        total = got_ref[mode * holders, :tiles, :].astype(F32)
        for holder in range(1, holders):
            total = total + got_ref[mode * holders + holder, :tiles, :].astype(F32)
        for part in range(2):
            block = total[part * half : (part + 1) * half]
            for piece in range(fold):
                stack[part].append(block[:, piece * bands : (piece + 1) * bands])
    matrix_high, matrix_low = split(jnp.concatenate(stack[0] + stack[1], axis=0))

    def product(x, y):
        return lax.dot_general(x, y, (((1,), (1,)), ((), ())), preferred_element_type=F32)

    folded = product(vector_high, matrix_high) + (
        product(vector_low, matrix_high) + product(vector_high, matrix_low)
    )
    side = modes * bands
    column = lax.broadcasted_iota(jnp.int32, (width, 2 * side), 1)
    sign = jnp.where(column < side, -1.0, 1.0)
    first = folded[:width] + sign * pltpu.roll(folded[width:], side, 1)
    second = pltpu.roll(first, side, 1) * -sign
    owner = (column % side) // bands
    left = [jnp.where(owner == mode, x, 0.0) for x in (first, second) for mode in range(modes)]
    left_high, left_low = split(jnp.concatenate(left, axis=0))
    for holder in range(holders):
        tile = [
            got_ref[group * holders + holder, tiles : tiles + share, :].astype(F32)
            for group in range(groups)
        ]
        tile = jnp.concatenate(tile, axis=0) if groups > 1 else tile[0]
        turned_ref[0, holder] = tile
        for turn in range(1, fold):
            turned_ref[turn, holder] = pltpu.roll(tile, turn * bands, 1)
    source = lax.broadcasted_iota(jnp.int32, (LANES, LANES), 0) % HALF
    target = lax.broadcasted_iota(jnp.int32, (LANES, LANES), 1) % bands
    spread = jnp.where(source == target, 1.0, 0.0).astype(BF16)
    rows = [got_ref[holder, begin : begin + 8, :] for holder in range(holders)]
    level_ref[...] = jnp.dot(
        jnp.concatenate(rows, axis=0), spread, preferred_element_type=F32
    ).reshape(level_ref.shape)
    span = queries * bands
    source = lax.broadcasted_iota(jnp.int32, (LANES, span), 0) % HALF
    target = lax.broadcasted_iota(jnp.int32, (LANES, span), 1) // bands
    spread = jnp.where(source == target, 1.0, 0.0).astype(BF16)
    down = lax.broadcasted_iota(jnp.int32, (width, bands), 0) + own_group * width
    across = lax.broadcasted_iota(jnp.int32, (width, bands), 1)
    energy = jnp.sum(jnp.where(down == across, energy_ref[...], 0.0), axis=1, keepdims=True)
    copy.wait()
    total = jnp.zeros((width, LANES), F32)
    for group in range(groups):
        table = jnp.dot(
            got_ref[group * holders, begin:, :], spread, preferred_element_type=F32
        )
        for start in range(0, queries, fold):
            points = [scalar_ref[group, 1, start + item] for item in range(fold)]
            level = level_ref[points[0]]
            for item in range(1, fold):
                level = jnp.where(slot == item, level_ref[points[item]], level)
            level = level[0:1]
            blocks = []
            for part in range(2):
                column = []
                for piece in range(fold):
                    rows = slice(part * half, (part + 1) * half)
                    block = turned_ref[(-piece) % fold, points[0], rows, :]
                    for item in range(1, fold):
                        block = jnp.where(
                            slot[:half] == item,
                            turned_ref[(item - piece) % fold, points[item], rows, :],
                            block,
                        )
                    column.append(block)
                blocks += column * modes
            chosen = jnp.concatenate(blocks, axis=0).astype(BF16)
            whole = jnp.dot(left_high, chosen, preferred_element_type=F32) + jnp.dot(
                left_low, chosen, preferred_element_type=F32
            )
            values = table[:, start * bands : (start + fold) * bands]
            fermi = 1.0 / (1.0 + jnp.exp(level / THERMAL))
            spacing = energy - level
            for out_mode in range(modes):
                real = imag = None
                for mode in range(modes):
                    row = 2 + modes * (1 + mode) + out_mode
                    weight = values[row : row + 1]
                    one = whole[mode * width : (mode + 1) * width] * weight
                    two = whole[(modes + mode) * width : (modes + mode + 1) * width] * weight
                    real = one if real is None else real + one
                    imag = two if imag is None else imag + two
                omega = values[2 + out_mode : 3 + out_mode]
                bose = 1.0 / (jnp.exp(omega / THERMAL) - 1.0)
                scale = SMEARING / math.pi
                up = spacing + omega
                off = spacing - omega
                up = up * up + SMEARING * SMEARING
                off = off * off + SMEARING * SMEARING
                absorb = (bose + fermi) * scale
                emit = (bose + 1.0 - fermi) * scale
                total = total + (real * real + imag * imag) * (absorb / up + emit / off)
    total = jnp.sum(total.T, axis=0, keepdims=True)
    out_ref[...] = total * (1.0 / (groups * queries))


def grant(size):
    return size + size // 4 + (2 << 20)


def shards(
    coupling, eigvec, energies, k_coords, r_coords, degeneracy, kq_index, omega, phonon_modes
):
    groups = lax.axis_size("pb")
    holders = lax.axis_size("ka")
    bands = energies.shape[1]
    queries = kq_index.shape[1]
    modes = omega.shape[1]
    slab = coupling.reshape(coupling.shape[0], -1)
    tiles = slab.shape[1] // LANES
    share = tiles // groups
    extra = -(-(share + 2 + modes * (modes + 1)) // 16) * 16 - share
    length = tiles + share + extra
    operands = (
        k_coords, r_coords, degeneracy, slab, eigvec.reshape(tiles, LANES),
        energies, kq_index, omega.T, phonon_modes.transpose(1, 2, 0),
    )
    operands = tuple(pltpu.with_memory_space_constraint(x, pltpu.HBM) for x in operands)
    parcel = pl.pallas_call(
        functools.partial(pack_kernel, groups),
        out_shape=jax.ShapeDtypeStruct((groups * holders, length, LANES), BF16),
        in_specs=[HBM] * 9,
        out_specs=VMEM,
        scratch_shapes=[
            pltpu.VMEM((holders * tiles, LANES), F32),
            pltpu.VMEM((extra, LANES), F32),
            *(pltpu.VMEM(x.shape, x.dtype) for x in operands),
            pltpu.SemaphoreType.DMA((9,)),
        ],
        compiler_params=pltpu.CompilerParams(
            vmem_limit_bytes=grant(2 * (slab.size + groups * holders * length * LANES))
            + 4 * holders * tiles * LANES
        ),
        name="pack",
    )(*operands)
    got = lax.all_to_all(parcel, ("pb", "ka"), 0, 0, tiled=True)
    return pl.pallas_call(
        functools.partial(energy_kernel, groups, bands, queries),
        out_shape=jax.ShapeDtypeStruct((1, bands // groups), F32),
        in_specs=[VMEM] * 3,
        out_specs=VMEM,
        scratch_shapes=[
            pltpu.VMEM((LANES // bands, holders, tiles, LANES), F32),
            pltpu.VMEM((holders, 8, LANES), F32),
            pltpu.VMEM((2, bands, LANES), F32),
            pltpu.VMEM((groups, 8, LANES), jnp.int32),
            pltpu.SMEM((groups, 8, LANES), jnp.int32),
            pltpu.SemaphoreType.DMA,
        ],
        compiler_params=pltpu.CompilerParams(
            vmem_limit_bytes=grant(
                2 * got.size + 4 * LANES * holders * (tiles * LANES // bands + 8)
            )
        ),
        name="energy",
    )(got, eigvec.reshape(tiles, LANES), energies)


def solution(mesh):
    in_specs = (
        P("ka", "pb", None),
        P("ka", None),
        P("ka", None),
        P(),
        P(None, "ka"),
        P("ka"),
        P("ka", "pb"),
        P("pb", None),
        P("pb", None, None),
    )
    out_specs = P("ka", "pb")
    return jax.shard_map(shards, mesh=mesh, in_specs=in_specs, out_specs=out_specs, check_vma=False)
```
